32 devices in a mesh: groups: 2 (over y), expert: 4 (over z), dp: 4 (over x, core).
Axes of the slice: x: 2, y: 2, z: 4, core: 2. Of those that a mesh axis runs over, the one named last changes fastest.
Arguments:
- tokens: bfloat16 [512, 6144], P(('groups', 'expert'), 'dp'), parts along dimension 0, may hold values from -6 to 6
- expert_ids: int32 [512, 8], P(('groups', 'expert')), parts along dimension 0, may hold values from 0 to 31, all different within a row; in each aligned block of 64 rows (0 to 63, 64 to 127, ...) at most 32 rows name the same one
- scores: float32 [512, 8], P(('groups', 'expert')), parts along dimension 0, may hold values from -8 to 8
- w_gate: bfloat16 [32, 6144, 1024], P('expert', 'dp'), may hold values from -0.078125 to 0.078125
- w_up: bfloat16 [32, 6144, 1024], P('expert', 'dp'), may hold values from -0.078125 to 0.078125
- w_down: bfloat16 [32, 1024, 6144], P('expert', None, 'dp'), may hold values from -0.1875 to 0.1875
Outputs:
- mixed: bfloat16 [512, 6144], P(('groups', 'expert'), 'dp'), parts along dimension 0
The draws below stay inside these ranges and needn't reach their ends.
There are 2 independent parts, one for each index of `groups`. The reference program is written for one: setup_inputs(seed, part) draws one part's arguments, and reference() takes and returns one part's arrays. A program takes and returns all parts, laid end to end along the dimension named above; an argument that names none is the same for every part. Nothing has to cross between parts.
Inputs may be any that keep to these rules, and one draw needn't show every extreme that they name: `expert_ids`: each row names 8 different experts; among the rows of one index of expert (aligned blocks of 64 rows) no expert is named by more than 32 rows, a bound that some block reaches.
All inputs are finite; a program needn't handle non-finite values.
Results may differ from the reference program's by a relative error of at most 0.024.
Values may be sent and summed in bfloat16 or wider, within the bound.
A program may use at most 128 MiB of HBM per device.

```python
import math
import jax
import jax.numpy as jnp
import numpy as np
from jax import lax

D = 6144
H = 1024
EXPERTS = 32
TOP = 8
TOK_DEV = 64
CAP = 32
TOKENS = 256
N_EXPERT = 4
N_DP = 4


def levels(own_key, dims, split, low, top_value):
    factor_of = 1.0
    for position, blocks in split:
        heights = jax.random.uniform(jax.random.fold_in(jax.random.fold_in(own_key, 6), position), (blocks,), jnp.float32, low / len(split), top_value / len(split))
        factor_of = factor_of * jnp.repeat(jnp.exp(heights), dims[position] // blocks).reshape((-1,) + (1,) * (len(dims) - 1 - position))
    return factor_of


def shared_out(rng, own, number, rows, number_of, top, limit, skew):
    order = jax.random.permutation(rng, number_of)
    packed, usual = load_shares(number_of, rows * top, limit, skew, True), load_shares(number_of, rows * top, limit, skew, False)
    places = jnp.arange(number_of)

    def named(tallies, offset_by):
        used = int((tallies > 0).sum())
        fixed = max(1, used // 4)
        moved = fixed + (places - fixed + offset_by * (used - fixed)) % max(1, number_of - fixed)
        return jnp.zeros((number_of,), jnp.int32).at[order[jnp.where(places < fixed, places, moved)]].set(jnp.asarray(tallies, jnp.int32))

    tallies = jnp.where(number % 4 == 0, named(packed, number // 4), named(usual, number - number // 4 - 1))
    mixed = jax.random.permutation(jax.random.fold_in(own, 3), number_of)
    donor, sink = mixed[0:number_of // 2 * 2:2], mixed[1:number_of // 2 * 2:2]
    room = jnp.minimum(tallies[donor] - 1, limit - tallies[sink]) // 2
    room = jnp.where((donor == order[0]) | (sink == order[0]) | (tallies[sink] == 0), 0, jnp.maximum(room, 0))
    moved = jax.random.randint(jax.random.fold_in(own, 4), (number_of // 2,), 0, 1 << 20) % (room + 1)
    tallies = tallies.at[donor].add(-moved).at[sink].add(moved)
    members = jnp.searchsorted(jnp.cumsum(tallies), jnp.arange(rows * top), side="right").astype(jnp.int32)
    grid = members.reshape(top, rows).T
    grid = grid[jax.random.permutation(jax.random.fold_in(own, 1), rows)]
    offset_by = jax.random.randint(jax.random.fold_in(own, 2), (rows, 1), 0, top)
    return jnp.take_along_axis(grid, (jnp.arange(top)[None, :] + offset_by) % top, axis=1)


def load_shares(count, total, limit, slope, full):
    weights = [(1 << 20) // math.isqrt(rank ** slope) + 1 for rank in range(1, count + 1)]
    largest = limit if full else min(limit, max(-(-total // count), total * weights[0] // sum(weights)))
    least = 1 if total - largest >= count - 1 else 0
    counts, spare = [largest] + [least] * (count - 1), total - largest - least * (count - 1)
    while spare > 0:
        movable = [i for i in range(1, count) if counts[i] < largest] or [i for i in range(1, count) if counts[i] < limit]
        whole, remaining = sum([weights[i] for i in movable]), spare
        for i in movable:
            more = min(limit - counts[i], max(1, remaining * weights[i] // whole), spare)
            counts[i] = counts[i] + more
            spare = spare - more
    return np.array(counts)


def bell_draw(stream_key, shape, deviation, most, split=(), kind=jnp.bfloat16):
    result = deviation * jax.random.normal(stream_key, shape, jnp.float32)
    if split:
        result = result * levels(stream_key, shape, split, -0.22, 0.18)
    return jnp.clip(result, -most, most).astype(kind)


def setup_inputs(seed: int = 0, part: int = 0) -> dict:
    keys = jax.random.split(jax.random.key(seed), 7)
    own_keys = jax.random.split(jax.random.fold_in(keys[6], part), 7)
    tokens = bell_draw(own_keys[0], (TOKENS, D), 1.0, 6.0, ((0, 4), (1, 4)))
    expert_ids_keys = jax.random.split(jax.random.fold_in(own_keys[1], 1), TOKENS // TOK_DEV)
    expert_ids_turns = jax.random.permutation(jax.random.fold_in(own_keys[1], 3), TOKENS // TOK_DEV)
    expert_ids = jax.vmap(lambda own, number: shared_out(jax.random.fold_in(own_keys[1], 2), own, number, TOK_DEV, EXPERTS, TOP, CAP, 2))(expert_ids_keys, expert_ids_turns).reshape((TOKENS, TOP))
    scores = bell_draw(own_keys[2], (TOKENS, TOP), 2.0, 8.0, ((0, 4),), jnp.float32)
    w_gate = bell_draw(keys[3], (EXPERTS, D, H), D ** -0.5, 0.078125, ((0, 4), (1, 4)))
    w_up = bell_draw(keys[4], (EXPERTS, D, H), D ** -0.5, 0.078125, ((0, 4), (1, 4)))
    w_down = bell_draw(keys[5], (EXPERTS, H, D), H ** -0.5, 0.1875, ((0, 4), (2, 4)))
    return dict(tokens=tokens, expert_ids=expert_ids, scores=scores, w_gate=w_gate, w_up=w_up, w_down=w_down)


def block_sum(parts, weight):
    local = D // N_DP
    blocks = jnp.einsum('rbd,bdh->rbh', parts, weight.reshape(N_DP, local, H).astype(jnp.float32))
    rounded = lax.optimization_barrier(blocks.astype(jnp.bfloat16))
    return jnp.sum(rounded.astype(jnp.float32), axis=1)


def reference(tokens, expert_ids, scores, w_gate, w_up, w_down):
    n_blocks = N_EXPERT
    ids = expert_ids.reshape(n_blocks, TOK_DEV * TOP)
    onehot = (ids[:, :, None] == jnp.arange(EXPERTS, dtype=jnp.int32)[None, None, :]).astype(jnp.int32)
    earlier = jnp.cumsum(onehot, axis=1) - onehot
    rank = jnp.sum(earlier * onehot, axis=2)
    block = jnp.arange(n_blocks, dtype=jnp.int32)[:, None]
    slots = ((ids * n_blocks + block) * CAP + rank).reshape(-1).astype(jnp.int32)
    source = jnp.repeat(jnp.arange(TOKENS, dtype=jnp.int32), TOP)
    buffer = jnp.zeros((EXPERTS * n_blocks * CAP, D), jnp.bfloat16).at[slots].set(tokens[source])
    buffer = buffer.reshape(EXPERTS, n_blocks * CAP, D)

    def expert_rows(items):
        rows, gate_w, up_w, down_w = items
        parts = rows.reshape(-1, N_DP, D // N_DP).astype(jnp.float32)
        gate = block_sum(parts, gate_w)
        up = block_sum(parts, up_w)
        hidden = (jax.nn.silu(gate) * up).astype(jnp.bfloat16)
        return jnp.dot(hidden, down_w, preferred_element_type=jnp.float32).astype(jnp.bfloat16)

    outputs = lax.map(expert_rows, (buffer, w_gate, w_up, w_down))
    picked = outputs.reshape(-1, D)[slots].reshape(TOKENS, TOP, D).astype(jnp.float32)
    affinity = jax.nn.sigmoid(scores)
    weights = 2.5 * affinity / jnp.sum(affinity, axis=1, keepdims=True)
    return jnp.einsum('tk,tkd->td', weights, picked).astype(jnp.bfloat16)
```

```python
import functools

import jax
import jax.numpy as jnp
from jax import lax
from jax.experimental import pallas as pl
from jax.experimental.pallas import tpu as pltpu
from jax.sharding import PartitionSpec as P

MESH = pl.DeviceIdType.MESH
F32, BF16 = jnp.float32, jnp.bfloat16
LAGS = (0, 1, 2, 3, 4)


def dot(a, b, dims=((1,), (0,))):
    return lax.dot_general(a, b, (dims, ((), ())), preferred_element_type=F32)


def remote(src, dst, send, recv, **where):
    return pltpu.make_async_remote_copy(
        src_ref=src, dst_ref=dst, send_sem=send, recv_sem=recv,
        device_id=where, device_id_type=MESH,
    )


def tile_of(size):
    for tile in (512, 384, 256, 128):
        if size % tile == 0:
            return tile
    return size


def kernel(dims, tok_ref, ids_ref, sco_ref, wg_hbm, wu_hbm, wd_hbm, out_ref,
           wg, wu, wd, xall, meta, slot_c, wgt_c, rows, s1, r1, keep, s2, r2, hid, acc,
           rs_s, rs_r, rs_l,
           wsem, ag_s, ag_r, p_s, p_r, q_s, q_r, h_s, h_r, f_s, f_r, t_s, t_r):
    E, DP, EL, NCH, G, CAP, NB = dims
    M = DP // 2
    tok, width = tok_ref.shape
    H = wg.shape[2]
    hb = H // DP
    R, T = G * CAP, G * tok
    N = EL * NCH
    ct = tile_of(width)
    e = lax.axis_index("expert")
    d = lax.axis_index("dp")
    x, c = lax.div(d, 2), lax.rem(d, 2)
    mate = 2 * x + 1 - c
    has_left, has_right = e > 0, e < E - 1

    def across(k):
        return lax.rem(x + k, M)

    def source(k):
        return lax.rem(x + M - k, M)

    def w_gu(j, slot):
        return (pltpu.make_async_copy(wg_hbm.at[j], wg.at[slot], wsem.at[0, slot]),
                pltpu.make_async_copy(wu_hbm.at[j], wu.at[slot], wsem.at[1, slot]))

    def w_d(j, slot):
        return pltpu.make_async_copy(wd_hbm.at[j], wd.at[slot], wsem.at[2, slot])

    for j in range(NB):
        for copy in w_gu(j, j):
            copy.start()
    for j in range(NB):
        w_d(j, j).start()

    barrier = pltpu.get_barrier_semaphore()

    @pl.when(has_left)
    def _():
        pl.semaphore_signal(barrier, inc=1, device_id={"expert": e - 1}, device_id_type=MESH)

    @pl.when(has_right)
    def _():
        pl.semaphore_signal(barrier, inc=1, device_id={"expert": e + 1}, device_id_type=MESH)

    pl.semaphore_signal(barrier, inc=1, device_id={"dp": mate}, device_id_type=MESH)
    for k in range(1, M):
        pl.semaphore_signal(
            barrier, inc=1, device_id={"dp": 2 * across(k) + c}, device_id_type=MESH)

    n_exp = E * EL
    affinity = 1.0 / (1.0 + jnp.exp(-sco_ref[...]))
    weights = 2.5 * affinity / jnp.sum(affinity, axis=0, keepdims=True)
    number = lax.broadcasted_iota(jnp.int32, (n_exp, tok), 0)
    routed = jnp.zeros((n_exp, tok), F32)
    weight = jnp.zeros((n_exp, tok), F32)
    for k in range(ids_ref.shape[0]):
        hit = ids_ref[k:k + 1, :] == number
        routed = routed + jnp.where(hit, 1.0, 0.0)
        weight = weight + jnp.where(hit, weights[k:k + 1, :], 0.0)
    earlier = (lax.broadcasted_iota(jnp.int32, (tok, tok), 0)
               < lax.broadcasted_iota(jnp.int32, (tok, tok), 1))
    rank = dot(routed.astype(BF16), jnp.where(earlier, 1.0, 0.0).astype(BF16))
    base = (lax.rem(e, G) * CAP).astype(F32)
    meta[e, :, :tok] = jnp.where(routed > 0.5, rank + base, -1.0)
    meta[e, :, tok:] = weight
    xall[e] = tok_ref[...]

    pl.semaphore_wait(barrier, M + has_left.astype(jnp.int32) + has_right.astype(jnp.int32))

    def gather_to(s, side, target):
        return (remote(meta.at[s], meta.at[s], ag_s.at[side, 0, s], ag_r.at[0, s], expert=target),
                remote(xall.at[s], xall.at[s], ag_s.at[side, 1, s], ag_r.at[1, s], expert=target))

    def start_right(s):
        @pl.when(has_right)
        def _():
            for copy in gather_to(s, 0, e + 1):
                copy.start()

    def start_left(s):
        @pl.when(has_left)
        def _():
            for copy in gather_to(s, 1, e - 1):
                copy.start()

    start_right(e)
    start_left(e)

    def gather_step(k, carry):
        @pl.when(e - k >= 0)
        def _():
            for copy in gather_to(e - k, 0, e):
                copy.wait_recv()
            start_right(e - k)

        @pl.when(e + k <= E - 1)
        def _():
            for copy in gather_to(e + k, 1, e):
                copy.wait_recv()
            start_left(e + k)

        return carry

    lax.fori_loop(1, E, gather_step, 0)

    for s in range(E):
        lanes = slice((s % G) * tok, (s % G + 1) * tok)
        own = meta[s, pl.ds(e * EL, EL), :]
        slot_c[s // G, :, lanes] = own[:, :tok]
        wgt_c[s // G, :, lanes] = own[:, tok:]
    acc[...] = jnp.zeros_like(acc)

    def split(i):
        if NCH == 1:
            return i, 0
        return lax.div(i, NCH), lax.rem(i, NCH)

    def taken(j, q):
        return (slot_c[q, pl.ds(j, 1), :]
                == lax.broadcasted_iota(jnp.int32, (R, T), 0).astype(F32))

    def pair_copy(i):
        return remote(s1.at[i], r1.at[i], p_s.at[i], p_r.at[i], dp=mate)

    def sum_copy(i, k):
        return remote(s2.at[i, across(k)], r2.at[i, x], q_s.at[i, k], q_r.at[i, k],
                      dp=2 * across(k) + c)

    def share_copy(i, k):
        return remote(hid.at[i, d], hid.at[i, d], h_s.at[i, k], h_r.at[i, k],
                      dp=2 * across(k) + c)

    def mate_copy(i, k):
        block = 2 * source(k) + c
        return remote(hid.at[i, block], hid.at[i, block], f_s.at[i, k], f_r.at[i, k], dp=mate)

    def stage_a(i):
        j, q = split(i)
        slot = lax.rem(j, NB)

        def load():
            for copy in w_gu(j, slot):
                copy.wait()

        if NCH == 1:
            load()
        else:
            pl.when(q == 0)(load)
        pick = jnp.where(taken(j, q), 1.0, 0.0).astype(BF16)
        for at in range(0, width, ct):
            xq = xall[pl.ds(q * G, G), :, at:at + ct].reshape(T, ct)
            rows[:, at:at + ct] = dot(pick, xq).astype(BF16)

        def block(m, core):
            cols = pl.ds(pl.multiple_of((2 * m + core) * hb, hb), hb)
            xr = rows[...]
            return dot(xr, wg[slot, :, cols]), dot(xr, wu[slot, :, cols])

        for m in range(M):
            g, u = block(m, 1 - c)
            s1[i, m, :, :hb] = g.astype(BF16)
            s1[i, m, :, hb:] = u.astype(BF16)
        pair_copy(i).start()
        for m in range(M):
            g, u = block(m, c)
            keep[i, m, :, :hb] = g
            keep[i, m, :, hb:] = u

        @pl.when((q == NCH - 1) & (j + NB < EL))
        def _():
            for copy in w_gu(j + NB, slot):
                copy.start()

    def stage_b(i):
        pair_copy(i).wait_recv()
        for k in range(1, M):
            to = across(k)
            s2[i, to] = (keep[i, to] + r1[i, to].astype(F32)).astype(BF16)
            sum_copy(i, k).start()
        keep[i, x] = keep[i, x] + r1[i, x].astype(F32)

    def stage_c(i):
        total = keep[i, x]
        for k in range(1, M):
            sum_copy(i, k).wait_recv()
            total = total + r2[i, source(k)].astype(F32)
        g, u = total[:, :hb], total[:, hb:]
        hid[i, d] = (g / (1.0 + jnp.exp(-g)) * u).astype(BF16)
        for k in range(1, M):
            share_copy(i, k).start()
        mate_copy(i, 0).start()

    def stage_d(i):
        for k in range(1, M):
            share_copy(i, k).wait_recv()
            mate_copy(i, k).start()

    def stage_e(i):
        j, q = split(i)
        slot = lax.rem(j, NB)

        def load():
            w_d(j, slot).wait()

        if NCH == 1:
            load()
        else:
            pl.when(q == 0)(load)
        for k in range(M):
            mate_copy(i, k).wait_recv()
        hit = taken(j, q)
        scale = jnp.sum(jnp.where(hit, wgt_c[q, pl.ds(j, 1), :], 0.0), axis=1, keepdims=True)
        pick = jnp.where(hit, 1.0, 0.0).astype(BF16)
        hidden = jnp.concatenate([hid[i, b] for b in range(DP)], axis=1)
        for at in range(0, width, ct):
            out = (dot(hidden, wd[slot, :, at:at + ct]) * scale).astype(BF16)
            add = dot(pick, out, ((0,), (0,))).reshape(G, tok, ct)
            acc[pl.ds(q * G, G), :, at:at + ct] += add

        @pl.when((q == NCH - 1) & (j + NB < EL))
        def _():
            w_d(j + NB, slot).start()

    stages = (stage_a, stage_b, stage_c, stage_d, stage_e)

    def step(i, carry):
        for stage, lag in zip(stages, LAGS):
            @pl.when((i >= lag) & (i < N + lag))
            def _(stage=stage, lag=lag):
                stage(i - lag)
        return carry

    lax.fori_loop(0, N + LAGS[-1], step, 0)

    def tail_right(s, target):
        return remote(rs_s.at[s], rs_r.at[s], t_s.at[s], t_r.at[0, s], expert=target)

    def tail_left(s, target):
        return remote(rs_s.at[s], rs_l.at[s], t_s.at[s], t_r.at[1, s], expert=target)

    def tail_step(t, carry):
        far, near = E - 1 - t, t

        @pl.when(far > e)
        def _():
            @pl.when(has_left)
            def _():
                tail_right(far, e).wait_recv()
                rs_s[far] = (acc[far] + rs_r[far].astype(F32)).astype(BF16)

            @pl.when(jnp.logical_not(has_left))
            def _():
                rs_s[far] = acc[far].astype(BF16)

            tail_right(far, e + 1).start()

        @pl.when(near < e)
        def _():
            @pl.when(has_right)
            def _():
                tail_left(near, e).wait_recv()
                rs_s[near] = (acc[near] + rs_l[near].astype(F32)).astype(BF16)

            @pl.when(jnp.logical_not(has_right))
            def _():
                rs_s[near] = acc[near].astype(BF16)

            tail_left(near, e - 1).start()

        return carry

    lax.fori_loop(0, E - 1, tail_step, 0)

    @pl.when(has_left)
    def _():
        tail_right(e, e).wait_recv()
        acc[e] = acc[e] + rs_r[e].astype(F32)

    @pl.when(has_right)
    def _():
        tail_left(e, e).wait_recv()
        acc[e] = acc[e] + rs_l[e].astype(F32)

    out_ref[...] = acc[e].astype(BF16)

    def drain_line(s, carry):
        @pl.when((s <= e) & has_right)
        def _():
            for copy in gather_to(s, 0, e):
                copy.wait_send()

        @pl.when((s >= e) & has_left)
        def _():
            for copy in gather_to(s, 1, e):
                copy.wait_send()

        @pl.when(s != e)
        def _():
            tail_right(s, e).wait_send()

        return carry

    lax.fori_loop(0, E, drain_line, 0)

    def drain_item(i, carry):
        pair_copy(i).wait_send()
        mate_copy(i, 0).wait_send()
        for k in range(1, M):
            sum_copy(i, k).wait_send()
            share_copy(i, k).wait_send()
            mate_copy(i, k).wait_send()
        return carry

    lax.fori_loop(0, N, drain_item, 0)


def on_device(tokens, expert_ids, scores, w_gate, w_up, w_down):
    E, DP = lax.axis_size("expert"), lax.axis_size("dp")
    tok, width = tokens.shape
    top = expert_ids.shape[1]
    EL, _, H = w_gate.shape
    n_exp = E * EL
    CAP = 2 * tok * top // n_exp
    G = min(E, 4)
    NCH = E // G
    NB = min(3, EL)
    M, hb, R, N = DP // 2, H // DP, G * CAP, EL * NCH
    vmem, dma = pltpu.VMEM, pltpu.SemaphoreType.DMA
    scratch = [
        vmem((NB, width, H), BF16), vmem((NB, width, H), BF16), vmem((NB, H, width), BF16),
        vmem((E, tok, width), BF16), vmem((E, n_exp, 2 * tok), F32),
        vmem((NCH, EL, G * tok), F32), vmem((NCH, EL, G * tok), F32),
        vmem((R, width), BF16),
        vmem((N, M, R, 2 * hb), BF16), vmem((N, M, R, 2 * hb), BF16),
        vmem((N, M, R, 2 * hb), F32),
        vmem((N, M, R, 2 * hb), BF16), vmem((N, M, R, 2 * hb), BF16),
        vmem((N, DP, R, hb), BF16),
        vmem((E, tok, width), F32),
        vmem((E, tok, width), BF16), vmem((E, tok, width), BF16), vmem((E, tok, width), BF16),
        dma((3, NB)), dma((2, 2, E)), dma((2, E)),
        dma((N,)), dma((N,)), dma((N, M)), dma((N, M)), dma((N, M)), dma((N, M)),
        dma((N, M)), dma((N, M)), dma((E,)), dma((2, E)),
    ]
    whole = pl.BlockSpec(memory_space=pltpu.VMEM)
    hbm = pl.BlockSpec(memory_space=pl.ANY)
    return pl.pallas_call(
        functools.partial(kernel, (E, DP, EL, NCH, G, CAP, NB)),
        out_shape=jax.ShapeDtypeStruct((tok, width), BF16),
        in_specs=[whole] * 3 + [hbm] * 3,
        out_specs=whole,
        scratch_shapes=scratch,
        compiler_params=pltpu.CompilerParams(
            collective_id=0, has_side_effects=True, vmem_limit_bytes=60 * 2**20),
        name="routed_experts",
    )(tokens, expert_ids.T, scores.T, w_gate, w_up, w_down)


def solution(mesh):
    in_specs = (
        P(("groups", "expert"), "dp"),
        P(("groups", "expert"), None),
        P(("groups", "expert"), None),
        P("expert", "dp", None),
        P("expert", "dp", None),
        P("expert", None, "dp"),
    )
    out_specs = P(("groups", "expert"), "dp")
    return jax.shard_map(
        on_device, mesh=mesh, in_specs=in_specs, out_specs=out_specs, check_vma=False
    )
```

```python
import functools

import jax
import jax.numpy as jnp
from jax import lax
from jax.experimental import pallas as pl
from jax.experimental.pallas import tpu as pltpu
from jax.sharding import PartitionSpec as P

MESH = pl.DeviceIdType.MESH
F32, BF16 = jnp.float32, jnp.bfloat16
LAGS = (0, 1, 2, 3, 4)


def dot(a, b, dims=((1,), (0,))):
    return lax.dot_general(a, b, (dims, ((), ())), preferred_element_type=F32)


def remote(src, dst, send, recv, **where):
    return pltpu.make_async_remote_copy(
        src_ref=src, dst_ref=dst, send_sem=send, recv_sem=recv,
        device_id=where, device_id_type=MESH,
    )


def tile_of(size):
    for tile in (512, 384, 256, 128):
        if size % tile == 0:
            return tile
    return size


def kernel(dims, tok_ref, ids_ref, sco_ref, wg_hbm, wu_hbm, wd_hbm, out_ref,
           wg, wu, wd, xall, meta, slot_c, wgt_c, rows, s1, r1, keep, s2, r2, hid, acc,
           rs_s, rs_r, rs_l,
           wsem, ag_s, ag_r, p_s, p_r, q_s, q_r, h_s, h_r, f_s, f_r, t_s, t_r):
    E, DP, EL, NCH, G, CAP, NB, HALF, CT = dims
    M = DP // 2
    tok, width = tok_ref.shape
    H = wg.shape[2]
    hb = H // DP
    R, T = G * CAP, G * tok
    N = EL * NCH
    ct = CT
    chunks = range(width // ct)
    n_items = N + 2 * HALF
    e = lax.axis_index("expert")
    d = lax.axis_index("dp")
    x, c = lax.div(d, 2), lax.rem(d, 2)
    mate = 2 * x + 1 - c
    has_left, has_right = e > 0, e < E - 1

    def place(s):
        return lax.rem(s + E // 4, E)

    def across(k):
        return lax.rem(x + k, M)

    def source(k):
        return lax.rem(x + M - k, M)

    def w_gu(j, slot):
        return (pltpu.make_async_copy(wg_hbm.at[j], wg.at[slot], wsem.at[0, slot]),
                pltpu.make_async_copy(wu_hbm.at[j], wu.at[slot], wsem.at[1, slot]))

    def w_d(j, slot):
        return pltpu.make_async_copy(wd_hbm.at[j], wd.at[slot], wsem.at[2, slot])

    for j in range(NB):
        for copy in w_gu(j, j):
            copy.start()
    for j in range(NB):
        w_d(j, j).start()

    barrier = pltpu.get_barrier_semaphore()

    @pl.when(has_left)
    def _():
        pl.semaphore_signal(barrier, inc=1, device_id={"expert": e - 1}, device_id_type=MESH)

    @pl.when(has_right)
    def _():
        pl.semaphore_signal(barrier, inc=1, device_id={"expert": e + 1}, device_id_type=MESH)

    pl.semaphore_signal(barrier, inc=1, device_id={"dp": mate}, device_id_type=MESH)
    for k in range(1, M):
        pl.semaphore_signal(
            barrier, inc=1, device_id={"dp": 2 * across(k) + c}, device_id_type=MESH)

    n_exp = E * EL
    affinity = 1.0 / (1.0 + jnp.exp(-sco_ref[...]))
    weights = 2.5 * affinity / jnp.sum(affinity, axis=0, keepdims=True)
    number = lax.broadcasted_iota(jnp.int32, (n_exp, tok), 0)
    routed = jnp.zeros((n_exp, tok), F32)
    weight = jnp.zeros((n_exp, tok), F32)
    for k in range(ids_ref.shape[0]):
        hit = ids_ref[k:k + 1, :] == number
        routed = routed + jnp.where(hit, 1.0, 0.0)
        weight = weight + jnp.where(hit, weights[k:k + 1, :], 0.0)
    earlier = (lax.broadcasted_iota(jnp.int32, (tok, tok), 0)
               < lax.broadcasted_iota(jnp.int32, (tok, tok), 1))
    rank = dot(routed.astype(BF16), jnp.where(earlier, 1.0, 0.0).astype(BF16))
    base = (place(e) * CAP).astype(F32)
    meta[e, :, :tok] = jnp.where(routed > 0.5, rank + base, -1.0)
    meta[e, :, tok:] = weight
    xall[place(e)] = tok_ref[...]

    pl.semaphore_wait(barrier, M + has_left.astype(jnp.int32) + has_right.astype(jnp.int32))

    def gather_to(s, side, target):
        return (remote(meta.at[s], meta.at[s], ag_s.at[side, 0, s], ag_r.at[0, s], expert=target),
                remote(xall.at[place(s)], xall.at[place(s)], ag_s.at[side, 1, s], ag_r.at[1, s], expert=target))

    def start_right(s):
        @pl.when(has_right)
        def _():
            for copy in gather_to(s, 0, e + 1):
                copy.start()

    def start_left(s):
        @pl.when(has_left)
        def _():
            for copy in gather_to(s, 1, e - 1):
                copy.start()

    start_right(e)
    start_left(e)

    def gather_step(k, carry):
        @pl.when(e - k >= 0)
        def _():
            for copy in gather_to(e - k, 0, e):
                copy.wait_recv()
            start_right(e - k)

        @pl.when(e + k <= E - 1)
        def _():
            for copy in gather_to(e + k, 1, e):
                copy.wait_recv()
            start_left(e + k)

        return carry

    def list_slots(places):
        for p in places:
            own = meta[(p + E - E // 4) % E, pl.ds(e * EL, EL), :]
            lanes = slice(p % 2 * tok, (p % 2 + 1) * tok)
            slot_c[p // 2, :, lanes] = own[:, :tok]
            wgt_c[p // 2, :, lanes] = own[:, tok:]

    if HALF:
        lax.fori_loop(1, 3 * E // 4, gather_step, 0)
        list_slots(range(E // 2, E))
    else:
        lax.fori_loop(1, E, gather_step, 0)
        list_slots(range(E))
    acc[...] = jnp.zeros_like(acc)

    class Item:
        def __init__(self, j, q, parts, first, last):
            self.j, self.q, self.first, self.last = j, q, first, last
            self.group = G // parts
            self.rows, self.toks = R // parts, T // parts
            self.start = q * self.group
            if parts == 1:
                self.buf = j if NCH == 1 else j * NCH + q
                self.sem = 2 * self.buf
                self.span = pl.ds(0, R)
            else:
                self.buf, self.sem = j, 2 * j + q
                self.span = pl.ds(pl.multiple_of(q * self.rows, self.rows), self.rows)
            self.places = pl.ds(self.start, self.group)

        def row(self, table):
            pairs = self.group // 2
            return jnp.concatenate(
                [table[self.q * pairs + p, pl.ds(self.j, 1), :] for p in range(pairs)], axis=1)

    def taken(it):
        row = it.row(slot_c)
        first = it.start * CAP
        return (row.astype(jnp.int32) - first
                == lax.broadcasted_iota(jnp.int32, (it.rows, it.toks), 0))

    def pair_copy(it):
        return remote(s1.at[it.buf, :, it.span], r1.at[it.buf, :, it.span],
                      p_s.at[it.sem], p_r.at[it.sem], dp=mate)

    def sum_copy(it, k):
        return remote(s2.at[it.buf, across(k), it.span], r2.at[it.buf, x, it.span],
                      q_s.at[it.sem, k], q_r.at[it.sem, k], dp=2 * across(k) + c)

    def share_copy(it, k):
        return remote(hid.at[it.buf, d, it.span], hid.at[it.buf, d, it.span],
                      h_s.at[it.sem, k], h_r.at[it.sem, k], dp=2 * across(k) + c)

    def mate_copy(it, k):
        block = 2 * source(k) + c
        return remote(hid.at[it.buf, block, it.span], hid.at[it.buf, block, it.span],
                      f_s.at[it.sem, k], f_r.at[it.sem, k], dp=mate)

    def stage_a(it):
        j, span = it.j, it.span
        slot = lax.rem(j, NB)

        @pl.when(it.first)
        def _():
            for copy in w_gu(j, slot):
                copy.wait()

        pick = jnp.where(taken(it), 1.0, 0.0).astype(BF16)
        for at in range(0, width, ct):
            xq = xall[it.places, :, at:at + ct].reshape(it.toks, ct)
            rows[:it.rows, at:at + ct] = dot(pick, xq).astype(BF16)

        def block(m, core):
            cols = pl.ds(pl.multiple_of((2 * m + core) * hb, hb), hb)
            xr = rows[:it.rows, :]
            return dot(xr, wg[slot, :, cols]), dot(xr, wu[slot, :, cols])

        for m in range(M):
            g, u = block(m, 1 - c)
            s1[it.buf, m, span, :hb] = g.astype(BF16)
            s1[it.buf, m, span, hb:] = u.astype(BF16)
        pair_copy(it).start()
        for m in range(M):
            g, u = block(m, c)
            keep[it.buf, m, span, :hb] = g
            keep[it.buf, m, span, hb:] = u

        @pl.when(it.last & (j + NB < EL))
        def _():
            for copy in w_gu(j + NB, slot):
                copy.start()

    def stage_b(it):
        i, span = it.buf, it.span
        pair_copy(it).wait_recv()
        for k in range(1, M):
            to = across(k)
            s2[i, to, span] = (keep[i, to, span] + r1[i, to, span].astype(F32)).astype(BF16)
            sum_copy(it, k).start()
        keep[i, x, span] = keep[i, x, span] + r1[i, x, span].astype(F32)

    def stage_c(it):
        i, span = it.buf, it.span
        total = keep[i, x, span]
        for k in range(1, M):
            sum_copy(it, k).wait_recv()
            total = total + r2[i, source(k), span].astype(F32)
        g, u = total[:, :hb], total[:, hb:]
        hid[i, d, span] = (g / (1.0 + jnp.exp(-g)) * u).astype(BF16)
        for k in range(1, M):
            share_copy(it, k).start()
        mate_copy(it, 0).start()

    def stage_d(it):
        for k in range(1, M):
            share_copy(it, k).wait_recv()
            mate_copy(it, k).start()

    def stage_e(it):
        j, span = it.j, it.span
        slot = lax.rem(j, NB)

        @pl.when(it.first)
        def _():
            w_d(j, slot).wait()

        for k in range(M):
            mate_copy(it, k).wait_recv()
        hit = taken(it)
        scale = jnp.sum(jnp.where(hit, it.row(wgt_c), 0.0),
                        axis=1, keepdims=True)
        pick = jnp.where(hit, 1.0, 0.0).astype(BF16)
        hidden = jnp.concatenate([hid[it.buf, b, span] for b in range(DP)], axis=1)
        for at in range(0, width, ct):
            out = (dot(hidden, wd[slot, :, at:at + ct]) * scale).astype(BF16)
            add = dot(pick, out, ((0,), (0,))).reshape(it.group, tok, ct)
            acc[it.places, :, at:at + ct] += add

        @pl.when(it.last & (j + NB < EL))
        def _():
            w_d(j + NB, slot).start()

    def tail_right(s, n, target):
        return remote(rs_s.at[s, n], rs_r.at[s, n], t_s.at[s, n], t_r.at[0, s, n], expert=target)

    def tail_left(s, n, target):
        return remote(rs_s.at[s, n], rs_l.at[s, n], t_s.at[s, n], t_r.at[1, s, n], expert=target)

    def first_sums(s, copy_to, target):
        for n in chunks:
            rs_s[s, n] = acc[place(s), :, n * ct:(n + 1) * ct].astype(BF16)
            copy_to(s, n, target).start()

    def outer_sums():
        @pl.when(jnp.logical_not(has_left))
        def _():
            first_sums(E - 1, tail_right, e + 1)

        @pl.when(jnp.logical_not(has_right))
        def _():
            first_sums(0, tail_left, e - 1)

    stages = (stage_a, stage_b, stage_c, stage_d, stage_e)

    n_ends = n_items - 2 * HALF

    def on_item(t, stage):
        if HALF == 0:
            if NCH == 1:
                stage(Item(t, 0, 1, t >= 0, t >= 0))
            else:
                q = lax.rem(t, NCH)
                stage(Item(lax.div(t, NCH), q, 1, q == 0, q == NCH - 1))
            return
        in_full = (t >= 2 * HALF) & (t < n_ends)

        @pl.when(in_full)
        def _():
            stage(Item(t - HALF, 0, 1, t >= 0, t >= 0))

        @pl.when(jnp.logical_not(in_full))
        def _():
            end = lax.div(t, n_ends)
            u = t - end * n_ends
            turn = lax.div(u, HALF)
            j = lax.rem(u, HALF) + end * (EL - HALF)
            q = end * turn + (1 - end) * (1 - turn)
            stage(Item(j, q, 2, turn == 0, turn == 1))

    def step(i, carry):
        if HALF:
            @pl.when(i == HALF)
            def _():
                lax.fori_loop(3 * E // 4, E, gather_step, 0)
                list_slots(range(E // 2))

        for stage, lag in zip(stages, LAGS):
            @pl.when((i >= lag) & (i < n_items + lag))
            def _(stage=stage, lag=lag):
                on_item(i - lag, stage)
        if HALF:
            @pl.when(i == n_items - HALF - 1 + LAGS[-1])
            def _():
                outer_sums()
        return carry

    lax.fori_loop(0, n_items + LAGS[-1], step, 0)

    if not HALF:
        outer_sums()

    def tail_step(t, carry):
        far, near = E - 1 - t, t
        for n in chunks:
            cols = slice(n * ct, (n + 1) * ct)

            @pl.when((far > e) & has_left)
            def _():
                tail_right(far, n, e).wait_recv()
                rs_s[far, n] = (acc[place(far), :, cols] + rs_r[far, n].astype(F32)).astype(BF16)
                tail_right(far, n, e + 1).start()

            @pl.when((far > e) & jnp.logical_not(has_left) & (t > 0))
            def _():
                rs_s[far, n] = acc[place(far), :, cols].astype(BF16)
                tail_right(far, n, e + 1).start()

            @pl.when((near < e) & has_right)
            def _():
                tail_left(near, n, e).wait_recv()
                rs_s[near, n] = (acc[place(near), :, cols]
                                 + rs_l[near, n].astype(F32)).astype(BF16)
                tail_left(near, n, e - 1).start()

            @pl.when((near < e) & jnp.logical_not(has_right) & (t > 0))
            def _():
                rs_s[near, n] = acc[place(near), :, cols].astype(BF16)
                tail_left(near, n, e - 1).start()

        return carry

    lax.fori_loop(0, E - 1, tail_step, 0)

    for n in chunks:
        cols = slice(n * ct, (n + 1) * ct)

        @pl.when(has_left)
        def _():
            tail_right(e, n, e).wait_recv()
            acc[place(e), :, cols] = acc[place(e), :, cols] + rs_r[e, n].astype(F32)

        @pl.when(has_right)
        def _():
            tail_left(e, n, e).wait_recv()
            acc[place(e), :, cols] = acc[place(e), :, cols] + rs_l[e, n].astype(F32)

        out_ref[:, cols] = acc[place(e), :, cols].astype(BF16)

    def drain_line(s, carry):
        @pl.when((s <= e) & has_right)
        def _():
            for copy in gather_to(s, 0, e):
                copy.wait_send()

        @pl.when((s >= e) & has_left)
        def _():
            for copy in gather_to(s, 1, e):
                copy.wait_send()

        @pl.when(s != e)
        def _():
            for n in chunks:
                tail_right(s, n, e).wait_send()

        return carry

    lax.fori_loop(0, E, drain_line, 0)

    def drain(it):
        pair_copy(it).wait_send()
        mate_copy(it, 0).wait_send()
        for k in range(1, M):
            sum_copy(it, k).wait_send()
            share_copy(it, k).wait_send()
            mate_copy(it, k).wait_send()

    def drain_item(t, carry):
        on_item(t, drain)
        return carry

    lax.fori_loop(0, n_items, drain_item, 0)


def on_device(tokens, expert_ids, scores, w_gate, w_up, w_down):
    E, DP = lax.axis_size("expert"), lax.axis_size("dp")
    tok, width = tokens.shape
    top = expert_ids.shape[1]
    EL, _, H = w_gate.shape
    n_exp = E * EL
    CAP = 2 * tok * top // n_exp
    G = min(E, 4)
    NCH = E // G
    NB = min(3, EL)
    HALF = 2 if NCH == 1 and G == 4 and EL > 4 else 0
    ct = tile_of(width)
    tail = (E, width // ct, tok, ct)
    M, hb, R, N = DP // 2, H // DP, G * CAP, EL * NCH
    vmem, dma = pltpu.VMEM, pltpu.SemaphoreType.DMA
    scratch = [
        vmem((NB, width, H), BF16), vmem((NB, width, H), BF16), vmem((NB, H, width), BF16),
        vmem((E, tok, width), BF16), vmem((E, n_exp, 2 * tok), F32),
        vmem((E // 2, EL, 2 * tok), F32), vmem((E // 2, EL, 2 * tok), F32),
        vmem((R, width), BF16),
        vmem((N, M, R, 2 * hb), BF16), vmem((N, M, R, 2 * hb), BF16),
        vmem((N, M, R, 2 * hb), F32),
        vmem((N, M, R, 2 * hb), BF16), vmem((N, M, R, 2 * hb), BF16),
        vmem((N, DP, R, hb), BF16),
        vmem((E, tok, width), F32),
        vmem(tail, BF16), vmem(tail, BF16), vmem(tail, BF16),
        dma((3, NB)), dma((2, 2, E)), dma((2, E)),
        dma((2 * N,)), dma((2 * N,)), dma((2 * N, M)), dma((2 * N, M)), dma((2 * N, M)),
        dma((2 * N, M)), dma((2 * N, M)), dma((2 * N, M)),
        dma((E, width // ct)), dma((2, E, width // ct)),
    ]
    whole = pl.BlockSpec(memory_space=pltpu.VMEM)
    hbm = pl.BlockSpec(memory_space=pl.ANY)
    return pl.pallas_call(
        functools.partial(kernel, (E, DP, EL, NCH, G, CAP, NB, HALF, ct)),
        out_shape=jax.ShapeDtypeStruct((tok, width), BF16),
        in_specs=[whole] * 3 + [hbm] * 3,
        out_specs=whole,
        scratch_shapes=scratch,
        compiler_params=pltpu.CompilerParams(
            collective_id=0, has_side_effects=True, vmem_limit_bytes=60 * 2**20),
        name="routed_experts",
    )(tokens, expert_ids.T, scores.T, w_gate, w_up, w_down)


def solution(mesh):
    in_specs = (
        P(("groups", "expert"), "dp"),
        P(("groups", "expert"), None),
        P(("groups", "expert"), None),
        P("expert", "dp", None),
        P("expert", "dp", None),
        P("expert", None, "dp"),
    )
    out_specs = P(("groups", "expert"), "dp")
    return jax.shard_map(
        on_device, mesh=mesh, in_specs=in_specs, out_specs=out_specs, check_vma=False
    )
```

```python
import functools

import jax
import jax.numpy as jnp
from jax import lax
from jax.experimental import pallas as pl
from jax.experimental.pallas import tpu as pltpu
from jax.sharding import PartitionSpec as P

MESH = pl.DeviceIdType.MESH
F32, BF16 = jnp.float32, jnp.bfloat16
LAGS = (0, 1, 3, 5, 7)


def dot(a, b, dims=((1,), (0,))):
    return lax.dot_general(a, b, (dims, ((), ())), preferred_element_type=F32)


def remote(src, dst, send, recv, **where):
    return pltpu.make_async_remote_copy(
        src_ref=src, dst_ref=dst, send_sem=send, recv_sem=recv,
        device_id=where, device_id_type=MESH,
    )


def tile_of(size):
    for tile in (512, 384, 256, 128):
        if size % tile == 0:
            return tile
    return size


def kernel(dims, tok_ref, ids_ref, sco_ref, wg_hbm, wu_hbm, wd_hbm, out_ref,
           wg, wu, wd, xall, meta, slot_c, wgt_c, rows, s1, r1, keep, s2, r2, hid, acc,
           rs_s, rs_r, rs_l,
           wsem, ag_s, ag_r, p_s, p_r, q_s, q_r, h_s, h_r, f_s, f_r, t_s, t_r):
    E, DP, EL, NCH, G, CAP, NB, HALF, CT, tw = dims
    M = DP // 2
    tok, width = tok_ref.shape
    H = wg.shape[2]
    hb = H // DP
    R, T = G * CAP, G * tok
    N = EL * NCH
    ct = CT
    chunks = range(width // tw)
    n_items = N + 2 * HALF
    e = lax.axis_index("expert")
    d = lax.axis_index("dp")
    x, c = lax.div(d, 2), lax.rem(d, 2)
    mate = 2 * x + 1 - c
    has_left, has_right = e > 0, e < E - 1

    def place(s):
        return lax.rem(s + E // 4, E)

    def across(k):
        return lax.rem(x + k, M)

    def source(k):
        return lax.rem(x + M - k, M)

    def w_gu(j, slot):
        return (pltpu.make_async_copy(wg_hbm.at[j], wg.at[slot], wsem.at[0, slot]),
                pltpu.make_async_copy(wu_hbm.at[j], wu.at[slot], wsem.at[1, slot]))

    def w_d(j, slot):
        return pltpu.make_async_copy(wd_hbm.at[j], wd.at[slot], wsem.at[2, slot])

    for j in range(NB):
        for copy in w_gu(j, j):
            copy.start()
    for j in range(NB):
        w_d(j, j).start()

    barrier = pltpu.get_barrier_semaphore()

    @pl.when(has_left)
    def _():
        pl.semaphore_signal(barrier, inc=1, device_id={"expert": e - 1}, device_id_type=MESH)

    @pl.when(has_right)
    def _():
        pl.semaphore_signal(barrier, inc=1, device_id={"expert": e + 1}, device_id_type=MESH)

    pl.semaphore_signal(barrier, inc=1, device_id={"dp": mate}, device_id_type=MESH)
    for k in range(1, M):
        pl.semaphore_signal(
            barrier, inc=1, device_id={"dp": 2 * across(k) + c}, device_id_type=MESH)

    n_exp = E * EL
    affinity = 1.0 / (1.0 + jnp.exp(-sco_ref[...]))
    weights = 2.5 * affinity / jnp.sum(affinity, axis=0, keepdims=True)
    number = lax.broadcasted_iota(jnp.int32, (n_exp, tok), 0)
    routed = jnp.zeros((n_exp, tok), F32)
    weight = jnp.zeros((n_exp, tok), F32)
    for k in range(ids_ref.shape[0]):
        hit = ids_ref[k:k + 1, :] == number
        routed = routed + jnp.where(hit, 1.0, 0.0)
        weight = weight + jnp.where(hit, weights[k:k + 1, :], 0.0)
    earlier = (lax.broadcasted_iota(jnp.int32, (tok, tok), 0)
               < lax.broadcasted_iota(jnp.int32, (tok, tok), 1))
    rank = dot(routed.astype(BF16), jnp.where(earlier, 1.0, 0.0).astype(BF16))
    base = (place(e) * CAP).astype(F32)
    meta[e, :, :tok] = jnp.where(routed > 0.5, rank + base, -1.0)
    meta[e, :, tok:] = weight
    xall[place(e)] = tok_ref[...]

    pl.semaphore_wait(barrier, M + has_left.astype(jnp.int32) + has_right.astype(jnp.int32))

    def gather_to(s, side, target):
        return (remote(meta.at[s], meta.at[s], ag_s.at[side, 0, s], ag_r.at[0, s], expert=target),
                remote(xall.at[place(s)], xall.at[place(s)], ag_s.at[side, 1, s], ag_r.at[1, s], expert=target))

    def start_right(s):
        @pl.when(has_right)
        def _():
            for copy in gather_to(s, 0, e + 1):
                copy.start()

    def start_left(s):
        @pl.when(has_left)
        def _():
            for copy in gather_to(s, 1, e - 1):
                copy.start()

    start_right(e)
    start_left(e)

    def gather_step(k, carry):
        @pl.when(e - k >= 0)
        def _():
            for copy in gather_to(e - k, 0, e):
                copy.wait_recv()
            start_right(e - k)

        @pl.when(e + k <= E - 1)
        def _():
            for copy in gather_to(e + k, 1, e):
                copy.wait_recv()
            start_left(e + k)

        return carry

    def list_slots(places):
        for p in places:
            own = meta[(p + E - E // 4) % E, pl.ds(e * EL, EL), :]
            lanes = slice(p % 2 * tok, (p % 2 + 1) * tok)
            slot_c[p // 2, :, lanes] = own[:, :tok]
            wgt_c[p // 2, :, lanes] = own[:, tok:]

    if HALF:
        lax.fori_loop(1, 3 * E // 4, gather_step, 0)
        list_slots(range(E // 2, E))
    else:
        lax.fori_loop(1, E, gather_step, 0)
        list_slots(range(E))
    acc[...] = jnp.zeros_like(acc)

    class Item:
        def __init__(self, j, q, parts, first, last):
            self.j, self.q, self.first, self.last = j, q, first, last
            self.group = G // parts
            self.rows, self.toks = R // parts, T // parts
            self.start = q * self.group
            if parts == 1:
                self.buf = j if NCH == 1 else j * NCH + q
                self.sem = 2 * self.buf
                self.span = pl.ds(0, R)
            else:
                self.buf, self.sem = j, 2 * j + q
                self.span = pl.ds(pl.multiple_of(q * self.rows, self.rows), self.rows)
            self.places = pl.ds(self.start, self.group)

        def row(self, table):
            pairs = self.group // 2
            return jnp.concatenate(
                [table[self.q * pairs + p, pl.ds(self.j, 1), :] for p in range(pairs)], axis=1)

    def taken(it):
        row = it.row(slot_c)
        first = it.start * CAP
        return (row.astype(jnp.int32) - first
                == lax.broadcasted_iota(jnp.int32, (it.rows, it.toks), 0))

    def pair_copy(it):
        return remote(s1.at[it.buf, :, it.span], r1.at[it.buf, :, it.span],
                      p_s.at[it.sem], p_r.at[it.sem], dp=mate)

    def sum_copy(it, k):
        return remote(s2.at[it.buf, across(k), it.span], r2.at[it.buf, x, it.span],
                      q_s.at[it.sem, k], q_r.at[it.sem, k], dp=2 * across(k) + c)

    def share_copy(it, k):
        return remote(hid.at[it.buf, d, it.span], hid.at[it.buf, d, it.span],
                      h_s.at[it.sem, k], h_r.at[it.sem, k], dp=2 * across(k) + c)

    def mate_copy(it, k):
        block = 2 * source(k) + c
        return remote(hid.at[it.buf, block, it.span], hid.at[it.buf, block, it.span],
                      f_s.at[it.sem, k], f_r.at[it.sem, k], dp=mate)

    def stage_a(it):
        j, span = it.j, it.span
        slot = lax.rem(j, NB)

        @pl.when(it.first)
        def _():
            for copy in w_gu(j, slot):
                copy.wait()

        pick = jnp.where(taken(it), 1.0, 0.0).astype(BF16)
        for at in range(0, width, ct):
            xq = xall[it.places, :, at:at + ct].reshape(it.toks, ct)
            rows[:it.rows, at:at + ct] = dot(pick, xq).astype(BF16)

        def block(m, core):
            cols = pl.ds(pl.multiple_of((2 * m + core) * hb, hb), hb)
            xr = rows[:it.rows, :]
            return dot(xr, wg[slot, :, cols]), dot(xr, wu[slot, :, cols])

        for m in range(M):
            g, u = block(m, 1 - c)
            s1[it.buf, m, span, :hb] = g.astype(BF16)
            s1[it.buf, m, span, hb:] = u.astype(BF16)
        pair_copy(it).start()
        for m in range(M):
            g, u = block(m, c)
            keep[it.buf, m, span, :hb] = g
            keep[it.buf, m, span, hb:] = u

        @pl.when(it.last & (j + NB < EL))
        def _():
            for copy in w_gu(j + NB, slot):
                copy.start()

    def stage_b(it):
        i, span = it.buf, it.span
        pair_copy(it).wait_recv()
        for k in range(1, M):
            to = across(k)
            s2[i, to, span] = (keep[i, to, span] + r1[i, to, span].astype(F32)).astype(BF16)
            sum_copy(it, k).start()
        keep[i, x, span] = keep[i, x, span] + r1[i, x, span].astype(F32)

    def stage_c(it):
        i, span = it.buf, it.span
        total = keep[i, x, span]
        for k in range(1, M):
            sum_copy(it, k).wait_recv()
            total = total + r2[i, source(k), span].astype(F32)
        g, u = total[:, :hb], total[:, hb:]
        hid[i, d, span] = (g / (1.0 + jnp.exp(-g)) * u).astype(BF16)
        for k in range(1, M):
            share_copy(it, k).start()
        mate_copy(it, 0).start()

    def stage_d(it):
        for k in range(1, M):
            share_copy(it, k).wait_recv()
            mate_copy(it, k).start()

    def stage_e(it):
        j, span = it.j, it.span
        slot = lax.rem(j, NB)

        @pl.when(it.first)
        def _():
            w_d(j, slot).wait()

        for k in range(M):
            mate_copy(it, k).wait_recv()
        hit = taken(it)
        scale = jnp.sum(jnp.where(hit, it.row(wgt_c), 0.0),
                        axis=1, keepdims=True)
        pick = jnp.where(hit, 1.0, 0.0).astype(BF16)
        hidden = jnp.concatenate([hid[it.buf, b, span] for b in range(DP)], axis=1)
        for at in range(0, width, ct):
            out = (dot(hidden, wd[slot, :, at:at + ct]) * scale).astype(BF16)
            add = dot(pick, out, ((0,), (0,))).reshape(it.group, tok, ct)
            acc[it.places, :, at:at + ct] += add

        @pl.when(it.last & (j + NB < EL))
        def _():
            w_d(j + NB, slot).start()

    def tail_right(s, n, target):
        return remote(rs_s.at[s, n], rs_r.at[s, n], t_s.at[s, n], t_r.at[0, s, n], expert=target)

    def tail_left(s, n, target):
        return remote(rs_s.at[s, n], rs_l.at[s, n], t_s.at[s, n], t_r.at[1, s, n], expert=target)

    def first_sums(s, copy_to, target):
        for n in chunks:
            rs_s[s, n] = acc[place(s), :, n * tw:(n + 1) * tw].astype(BF16)
            copy_to(s, n, target).start()

    def outer_sums():
        @pl.when(jnp.logical_not(has_left))
        def _():
            first_sums(E - 1, tail_right, e + 1)

        @pl.when(jnp.logical_not(has_right))
        def _():
            first_sums(0, tail_left, e - 1)

    stages = (stage_a, stage_b, stage_c, stage_d, stage_e)

    n_ends = n_items - 2 * HALF

    def on_item(t, stage):
        if HALF == 0:
            if NCH == 1:
                stage(Item(t, 0, 1, t >= 0, t >= 0))
            else:
                q = lax.rem(t, NCH)
                stage(Item(lax.div(t, NCH), q, 1, q == 0, q == NCH - 1))
            return
        in_full = (t >= 2 * HALF) & (t < n_ends)

        @pl.when(in_full)
        def _():
            stage(Item(t - HALF, 0, 1, t >= 0, t >= 0))

        @pl.when(jnp.logical_not(in_full))
        def _():
            end = lax.div(t, n_ends)
            u = t - end * n_ends
            turn = lax.div(u, HALF)
            j = lax.rem(u, HALF) + end * (EL - HALF)
            q = end * turn + (1 - end) * (1 - turn)
            stage(Item(j, q, 2, turn == 0, turn == 1))

    def step(i, carry):
        if HALF:
            @pl.when(i == HALF)
            def _():
                lax.fori_loop(3 * E // 4, E, gather_step, 0)
                list_slots(range(E // 2))

        for stage, lag in zip(stages, LAGS):
            @pl.when((i >= lag) & (i < n_items + lag))
            def _(stage=stage, lag=lag):
                on_item(i - lag, stage)
        if HALF:
            @pl.when(i == n_items - HALF - 1 + LAGS[-1])
            def _():
                outer_sums()
        return carry

    lax.fori_loop(0, n_items + LAGS[-1], step, 0)

    if not HALF:
        outer_sums()

    def tail_step(t, carry):
        far, near = E - 1 - t, t
        for n in chunks:
            cols = slice(n * tw, (n + 1) * tw)

            @pl.when((far > e) & has_left)
            def _():
                tail_right(far, n, e).wait_recv()
                rs_s[far, n] = (acc[place(far), :, cols] + rs_r[far, n].astype(F32)).astype(BF16)
                tail_right(far, n, e + 1).start()

            @pl.when((far > e) & jnp.logical_not(has_left) & (t > 0))
            def _():
                rs_s[far, n] = acc[place(far), :, cols].astype(BF16)
                tail_right(far, n, e + 1).start()

            @pl.when((near < e) & has_right)
            def _():
                tail_left(near, n, e).wait_recv()
                rs_s[near, n] = (acc[place(near), :, cols]
                                 + rs_l[near, n].astype(F32)).astype(BF16)
                tail_left(near, n, e - 1).start()

            @pl.when((near < e) & jnp.logical_not(has_right) & (t > 0))
            def _():
                rs_s[near, n] = acc[place(near), :, cols].astype(BF16)
                tail_left(near, n, e - 1).start()

        return carry

    lax.fori_loop(0, E - 1, tail_step, 0)

    for n in chunks:
        cols = slice(n * tw, (n + 1) * tw)

        @pl.when(has_left)
        def _():
            tail_right(e, n, e).wait_recv()
            acc[place(e), :, cols] = acc[place(e), :, cols] + rs_r[e, n].astype(F32)

        @pl.when(has_right)
        def _():
            tail_left(e, n, e).wait_recv()
            acc[place(e), :, cols] = acc[place(e), :, cols] + rs_l[e, n].astype(F32)

        out_ref[:, cols] = acc[place(e), :, cols].astype(BF16)

    def drain_line(s, carry):
        @pl.when((s <= e) & has_right)
        def _():
            for copy in gather_to(s, 0, e):
                copy.wait_send()

        @pl.when((s >= e) & has_left)
        def _():
            for copy in gather_to(s, 1, e):
                copy.wait_send()

        @pl.when(s != e)
        def _():
            for n in chunks:
                tail_right(s, n, e).wait_send()

        return carry

    lax.fori_loop(0, E, drain_line, 0)

    def drain(it):
        pair_copy(it).wait_send()
        mate_copy(it, 0).wait_send()
        for k in range(1, M):
            sum_copy(it, k).wait_send()
            share_copy(it, k).wait_send()
            mate_copy(it, k).wait_send()

    def drain_item(t, carry):
        on_item(t, drain)
        return carry

    lax.fori_loop(0, n_items, drain_item, 0)


def on_device(tokens, expert_ids, scores, w_gate, w_up, w_down):
    E, DP = lax.axis_size("expert"), lax.axis_size("dp")
    tok, width = tokens.shape
    top = expert_ids.shape[1]
    EL, _, H = w_gate.shape
    n_exp = E * EL
    CAP = 2 * tok * top // n_exp
    G = min(E, 4)
    NCH = E // G
    NB = min(3, EL)
    HALF = 2 if NCH == 1 and G == 4 and EL > 4 else 0
    ct = tile_of(width)
    tw = width
    tail = (E, width // tw, tok, tw)
    M, hb, R, N = DP // 2, H // DP, G * CAP, EL * NCH
    vmem, dma = pltpu.VMEM, pltpu.SemaphoreType.DMA
    scratch = [
        vmem((NB, width, H), BF16), vmem((NB, width, H), BF16), vmem((NB, H, width), BF16),
        vmem((E, tok, width), BF16), vmem((E, n_exp, 2 * tok), F32),
        vmem((E // 2, EL, 2 * tok), F32), vmem((E // 2, EL, 2 * tok), F32),
        vmem((R, width), BF16),
        vmem((N, M, R, 2 * hb), BF16), vmem((N, M, R, 2 * hb), BF16),
        vmem((N, M, R, 2 * hb), F32),
        vmem((N, M, R, 2 * hb), BF16), vmem((N, M, R, 2 * hb), BF16),
        vmem((N, DP, R, hb), BF16),
        vmem((E, tok, width), F32),
        vmem(tail, BF16), vmem(tail, BF16), vmem(tail, BF16),
        dma((3, NB)), dma((2, 2, E)), dma((2, E)),
        dma((2 * N,)), dma((2 * N,)), dma((2 * N, M)), dma((2 * N, M)), dma((2 * N, M)),
        dma((2 * N, M)), dma((2 * N, M)), dma((2 * N, M)),
        dma((E, width // tw)), dma((2, E, width // tw)),
    ]
    whole = pl.BlockSpec(memory_space=pltpu.VMEM)
    hbm = pl.BlockSpec(memory_space=pl.ANY)
    return pl.pallas_call(
        functools.partial(kernel, (E, DP, EL, NCH, G, CAP, NB, HALF, ct, tw)),
        out_shape=jax.ShapeDtypeStruct((tok, width), BF16),
        in_specs=[whole] * 3 + [hbm] * 3,
        out_specs=whole,
        scratch_shapes=scratch,
        compiler_params=pltpu.CompilerParams(
            collective_id=0, has_side_effects=True, vmem_limit_bytes=60 * 2**20),
        name="routed_experts",
    )(tokens, expert_ids.T, scores.T, w_gate, w_up, w_down)


def solution(mesh):
    in_specs = (
        P(("groups", "expert"), "dp"),
        P(("groups", "expert"), None),
        P(("groups", "expert"), None),
        P("expert", "dp", None),
        P("expert", "dp", None),
        P("expert", None, "dp"),
    )
    out_specs = P(("groups", "expert"), "dp")
    return jax.shard_map(
        on_device, mesh=mesh, in_specs=in_specs, out_specs=out_specs, check_vma=False
    )
```
